256 devices in a mesh: sec: 64 (over z, x, core), op: 4 (over y).
Axes of the slice: x: 4, y: 4, z: 8, core: 2. Of those that a mesh axis runs over, the one named last changes fastest.
Arguments:
- wavefunction: bfloat16 [4096, 128, 128], P('sec'), may hold values from -6 to 6
- sector_left: int32 [4096], P('sec'), may hold values from 0 to 127, as said below
- sector_right: int32 [4096], replicated, may hold values from 0 to 127, as said below
- left_sizes: int32 [128], replicated, may hold values from 64 to 128
- right_sizes: int32 [128], replicated, may hold values from 64 to 128
- term_mask: int32 [16, 4096], P('op', 'sec'), may hold values 0 or 1
- left_environment: bfloat16 [16, 128, 128, 128], P('op', 'sec'), may hold values from -0.5 to 0.5
- right_environment: bfloat16 [16, 128, 128, 128], P('op', 'sec'), may hold values from -0.5 to 0.5
- krylov_basis: bfloat16 [4, 4096, 128, 128], P(None, 'sec', 'op')
Outputs:
- applied_wave: bfloat16 [4096, 128, 128], P('sec', 'op')
- correlations: float32 [4], replicated
The draws below stay inside these ranges and needn't reach their ends.
Inputs may be any that keep to these rules, and one draw needn't show every extreme that they name: `sector_left`: sector s has one of the 2 left numbers 2 * (s // 64) to 2 * (s // 64) + 1. `sector_right`: right number q is owned by index q // 2 of sec. No two sectors among the 64 of one device share a right number; at most 2 of them share a right owner, and in every draw some owner receives 2 sectors from every device. Right numbers 0 to 127 are drawn, and 127 is used in every draw.
All inputs are finite; a program needn't handle non-finite values. No bound on the sum of `term_mask` on one device may be relied on, other than what follows from the above.
Results may differ from the reference program's by a relative error of at most 0.0049.
Values may be sent and summed in bfloat16 or wider, within the bound.
A program may use at most 256 MiB of HBM per device.

```python
import math
import jax
import jax.numpy as jnp
from jax import lax

B = 128
WB = 16
LQ_DEV = 2
RQ_DEV = 2
CAP = 2
K = 4
HOLDERS = 64
SEC_DEV = 64
NSECT = 4096
NLQ = 128
NRQ = 128


def draw_sector_left(key, part):
    inner_key = jax.random.fold_in(key, 11)
    offset = jax.random.randint(inner_key, (NSECT,), 0, LQ_DEV)
    return (offset + LQ_DEV * (jnp.arange(NSECT) // SEC_DEV)).astype(jnp.int32)


def draw_sector_right(key, part):
    inner_key = jax.random.fold_in(key, 23)
    weight_key, favour_key, score_key = jax.random.split(inner_key, 3)
    slot_total = HOLDERS * CAP
    weights = jax.random.randint(weight_key, (HOLDERS,), 0, 3)
    favoured = jax.random.randint(favour_key, (), 0, HOLDERS)
    weights = jnp.where(jnp.arange(HOLDERS) == favoured, 3, weights)
    slot_weight = jnp.repeat(weights, CAP)
    slot_range = jnp.arange(slot_total)

    def device_pick(device_key, device_number):
        noise = jax.random.randint(device_key, (slot_total,), 0, 1024)
        boosted = (device_number == 0) & (slot_range == slot_total - 1)
        weight_here = jnp.where(boosted, 4, slot_weight)
        score = (weight_here * 1024 + noise) * slot_total + slot_range
        best, chosen = lax.top_k(score, SEC_DEV)
        return jnp.sort(chosen)
    picked = jax.vmap(device_pick)(jax.random.split(score_key, HOLDERS), jnp.arange(HOLDERS))
    owner = picked // CAP
    within = picked % CAP
    return (owner * RQ_DEV + within).reshape(-1).astype(jnp.int32)


def sized_blocks(key, count):
    value_key, index_key = jax.random.split(key)
    values = jax.random.randint(value_key, (count,), B // 2, B + 1)
    chosen = jax.random.randint(index_key, (), 0, count)
    return jnp.where(jnp.arange(count) == chosen, B, values).astype(jnp.int32)


def draw_left_sizes(key, part):
    return sized_blocks(jax.random.fold_in(key, 31), NLQ)


def draw_right_sizes(key, part):
    return sized_blocks(jax.random.fold_in(key, 37), NRQ)


def draw_krylov_basis(key, part):
    inner_key = jax.random.fold_in(key, 41)
    position = jnp.arange(NSECT, dtype=jnp.float32) / NSECT
    raw = jax.random.normal(inner_key, (K, NSECT, B, B))
    scale = 3.0 ** position
    return (raw * scale[None, :, None, None] / math.sqrt(NSECT * B * B)).astype(jnp.bfloat16)


def with_ends(array, own_key, low, largest):
    longest = array.shape.index(max(array.shape))
    spots = []
    for shift in (0, 1):
        where = [jax.random.randint(jax.random.fold_in(own_key, axis), (), 0, length) for axis, length in enumerate(array.shape)]
        where[longest] = (where[longest] + shift) % array.shape[longest]
        spots.append(tuple(where))
    return array.at[spots[0]].set(low).at[spots[1]].set(largest)


def block_scale(key, dims, cuts, low, high):
    def one(axis_at, shards_of):
        draws = jax.random.uniform(jax.random.fold_in(jax.random.fold_in(key, 6), axis_at), (shards_of,), jnp.float32, low / len(cuts), high / len(cuts))
        return jnp.repeat(jnp.exp(draws), dims[axis_at] // shards_of).reshape((-1,) + (1,) * (len(dims) - axis_at - 1))

    level = one(*cuts[0])
    for cut in cuts[1:]:
        level = level * one(*cut)
    return level


def bell_draw(key, dims, scale, most, cuts=(), kind=jnp.bfloat16):
    factor_of = block_scale(key, dims, cuts, -0.22, 0.18) if cuts else 1.0
    entries = jax.random.normal(key, dims, jnp.float32) * scale * factor_of
    return jnp.minimum(jnp.maximum(entries, -most), most).astype(kind)


def setup_inputs(seed: int = 0) -> dict:
    keys = jax.random.split(jax.random.key(seed), 10)
    wavefunction = bell_draw(keys[0], (NSECT, B, B), 1.0, 6.0, ((0, 64),))
    sector_left = draw_sector_left(jax.random.fold_in(keys[9], 71), 0)
    sector_right = draw_sector_right(jax.random.fold_in(keys[9], 71), 0)
    left_sizes = draw_left_sizes(jax.random.fold_in(keys[9], 71), 0)
    right_sizes = draw_right_sizes(jax.random.fold_in(keys[9], 71), 0)
    term_mask = with_ends((jax.random.randint(keys[5], (WB, NSECT), 0, 2) < 1).astype(jnp.int32), jax.random.fold_in(keys[5], 1), 0, 1)
    left_environment = bell_draw(keys[6], (WB, NLQ, B, B), B ** -0.5, 0.5, ((0, 4), (1, 64)))
    right_environment = bell_draw(keys[7], (WB, NRQ, B, B), B ** -0.5, 0.5, ((0, 4), (1, 64)))
    krylov_basis = draw_krylov_basis(jax.random.fold_in(keys[9], 71), 0)
    return dict(wavefunction=wavefunction, sector_left=sector_left, sector_right=sector_right, left_sizes=left_sizes, right_sizes=right_sizes, term_mask=term_mask, left_environment=left_environment, right_environment=right_environment, krylov_basis=krylov_basis)


def reference(wavefunction, sector_left, sector_right, left_sizes, right_sizes, term_mask, left_environment, right_environment, krylov_basis):
    lane_index = jnp.arange(B, dtype=jnp.int32)

    def sector_product(pieces):
        tile_block, left_number, right_number, mask_column = pieces
        rows_inside = (lane_index < left_sizes[left_number]).astype(jnp.float32)
        cols_inside = (lane_index < right_sizes[right_number]).astype(jnp.float32)
        masked_psi = (tile_block.astype(jnp.float32) * rows_inside[:, None] * cols_inside[None, :]).astype(jnp.bfloat16)
        left_tiles = lax.dynamic_index_in_dim(left_environment, left_number, 1, keepdims=False)
        right_tiles = lax.dynamic_index_in_dim(right_environment, right_number, 1, keepdims=False)
        left_part = jnp.einsum('wij,jk->wik', left_tiles.astype(jnp.float32), masked_psi.astype(jnp.float32))
        left_part = (left_part * rows_inside[None, :, None] * mask_column[:, None, None]).astype(jnp.bfloat16)
        summed = jnp.einsum('wij,wkj->ik', left_part.astype(jnp.float32), right_tiles.astype(jnp.float32))
        return (summed * cols_inside[None, :]).astype(jnp.bfloat16)

    applied_wave = lax.map(sector_product, (wavefunction, sector_left, sector_right, term_mask.T.astype(jnp.float32)))
    wave_float = applied_wave.astype(jnp.float32)

    def inner_product(vector):
        return jnp.sum(vector.astype(jnp.float32) * wave_float)

    correlations = lax.map(inner_product, krylov_basis)
    return applied_wave, correlations
```

```python
import jax
import jax.numpy as jnp
from jax import lax
from jax.sharding import PartitionSpec as P


def lookup_small(keys, table):
    table_index = jnp.arange(table.shape[0], dtype=jnp.int32)
    return jnp.sum(jnp.where(keys[:, None] == table_index[None, :], table[None, :], 0), axis=1)


def per_device(
    wavefunction,
    sector_left,
    sector_right,
    left_sizes,
    right_sizes,
    term_mask,
    left_environment,
    right_environment,
    krylov_basis,
):
    holder = lax.axis_index("sec")
    parts = lax.axis_size("op")
    sector_count = wavefunction.shape[0]
    tile_size = wavefunction.shape[1]
    left_per = left_environment.shape[1]
    my_right = lax.dynamic_slice_in_dim(sector_right, holder * sector_count, sector_count)
    everything = lax.all_gather(right_environment, "sec", axis=1, tiled=True)
    lane_index = jnp.arange(tile_size, dtype=jnp.int32)
    left_size = lookup_small(sector_left, left_sizes)
    right_size = lookup_small(my_right, right_sizes)
    rows_inside = lane_index[None, :] < left_size[:, None]
    cols_inside = lane_index[None, :] < right_size[:, None]
    inside = rows_inside[:, :, None] & cols_inside[:, None, :]
    masked_psi = jnp.where(inside, wavefunction, jnp.zeros((), jnp.bfloat16))
    left_index = sector_left - holder * left_per
    left_tiles = jnp.take(left_environment, left_index, axis=1)
    product = jnp.einsum(
        "wsij,sjk->swik", left_tiles, masked_psi, preferred_element_type=jnp.float32
    )
    term_weight = term_mask.T.astype(jnp.float32)[:, :, None, None]
    row_weight = rows_inside.astype(jnp.float32)[:, None, :, None]
    left_part = (product * term_weight * row_weight).astype(jnp.bfloat16)
    env_tiles = jnp.take(everything, my_right, axis=1)
    partial_value = jnp.einsum(
        "swij,wskj->sik", left_part, env_tiles, preferred_element_type=jnp.float32
    ).astype(jnp.bfloat16)
    shares = partial_value.reshape(sector_count, parts, tile_size // parts, tile_size)
    shares = lax.all_to_all(shares, "op", split_axis=1, concat_axis=1, tiled=True)
    result_rows = jnp.sum(shares.astype(jnp.float32), axis=1)
    applied_wave = jnp.where(cols_inside[:, None, :], result_rows, 0.0).astype(jnp.bfloat16)
    local_sum = jnp.einsum(
        "ksij,sij->k", krylov_basis, applied_wave, preferred_element_type=jnp.float32
    )
    correlations = lax.psum(local_sum, ("sec", "op"))
    return (applied_wave, correlations)


def solution(mesh):
    return jax.shard_map(
        per_device,
        mesh=mesh,
        in_specs=(
            P("sec", None, None),
            P("sec"),
            P(),
            P(),
            P(),
            P("op", "sec"),
            P("op", "sec", None, None),
            P("op", "sec", None, None),
            P(None, "sec", "op", None),
        ),
        out_specs=(P("sec", "op", None), P()),
        check_vma=False,
    )
```

```python
import jax
import jax.numpy as jnp
from jax import lax
from jax.experimental import pallas as pl
from jax.experimental.pallas import tpu as pltpu
from jax.sharding import PartitionSpec as P

MESH = pl.DeviceIdType.MESH
NZ, NX, NC, NY = 8, 4, 2, 4
TILE = 128
HALF = 1024
BLOCK = 2 * HALF
SPLIT = {"A": (0, 208), "B": (416, 304)}
GROUP = 4

ORDER = (
    (0, 0), (-1, 0), (0, -1), (0, 1),
    (1, 0), (-2, 0), (-1, -1), (1, -1),
    (1, 1), (0, 2), (-1, 1), (2, 0),
    (-3, 0), (2, -1), (-2, -1), (2, 1),
    (-1, 2), (1, 2), (-2, 1), (3, 0),
    (-3, -1), (3, -1), (3, 1), (-2, 2),
    (2, 2), (-3, 1), (4, 0), (4, -1),
    (-3, 2), (3, 2), (4, 1), (4, 2),
)

PLAN = (
    (("B", 0), ("A", 0),),
    (("B", 1), ("B", 2), ("B", 3), ("B", 4), ("A", 1), ("A", 2), ("A", 3), ("A", 4),),
    (),
    (),
    (("B", 5), ("B", 6), ("B", 10), ("B", 11),),
    (("B", 9), ("A", 5), ("A", 7),),
    (("A", 6), ("A", 8), ("B", 7), ("B", 8),),
    (("A", 9), ("A", 10), ("A", 11),),
    (),
    (),
    (),
    (("B", 14), ("B", 18), ("B", 12), ("B", 19),),
    (("B", 16), ("A", 12), ("A", 13),),
    (("B", 13), ("B", 15), ("A", 14), ("A", 15), ("B", 17),),
    (),
    (("A", 16), ("A", 17), ("B", 23),),
    (),
    (("A", 18), ("A", 19),),
    (("B", 26), ("B", 20), ("B", 25),),
    (),
    (("A", 21), ("A", 20), ("B", 21), ("B", 22), ("A", 22),),
    (("B", 24), ("A", 23),),
    (),
    (("A", 24),),
    (("A", 25), ("A", 26), ("B", 27), ("B", 30),),
    (("A", 27),),
    (("B", 28),),
    (),
    (("A", 28), ("B", 29), ("A", 29), ("A", 30), ("B", 31),),
    (),
    (),
    (("A", 31),),
)

SLOT = {place: index for index, place in enumerate(ORDER)}
BLOCKS = len(ORDER)


def onward(kind, dz, dx):
    out = []
    along_z = kind == "A" or dx == 0
    along_x = kind == "B" or dz == 0
    if along_z:
        if -3 <= dz <= 0:
            out.append(("z+", 2 if dz > -3 else 0, (dz - 1 if dz > -3 else 4, dx)))
        if 0 <= dz <= 3:
            out.append(("z-", 2 if dz < 3 else 1, (dz + 1, dx)))
    if along_x:
        if -1 <= dx <= 0:
            out.append(("x+", 2 if dx == 0 else 0, (dz, -1 if dx == 0 else 2)))
        if 0 <= dx <= 1:
            out.append(("x-", 2 if dx == 0 else 1, (dz, dx + 1)))
    return out


def piece(kind, slot, parts):
    first, rows = SPLIT[kind]
    start = slot * BLOCK + first + (rows if parts == 1 else 0)
    return pl.ds(start, 2 * rows if parts == 2 else rows)


def kernel(
    tab, lenv, rpre, tmask, psi_hbm, kry_hbm,
    applied, corr,
    rbuf, psi, kry, lall, tmall, outb, recvb, sums, gather_z, gather_x, gather_y,
    load_sem, pre_sem, pre_send, side_sem, side_send, a_sem, b_sem, twin_sem, twin_send, link_send,
    out_sem, out_send, own_sem, sum_sem, sum_send,
):
    sec = lax.axis_index("sec")
    y = lax.axis_index("op")
    z = sec // (NX * NC)
    x = (sec // NC) % NX
    core = sec % NC

    def device(dz=0, dx=0, dc=0, dy=0):
        at_z = lax.rem(z + dz + NZ, NZ) if dz else z
        at_x = lax.rem(x + dx + NX, NX) if dx else x
        at_c = 1 - core if dc else core
        at_y = lax.rem(y + dy + NY, NY) if dy else y
        return {"sec": (at_z * NX + at_x) * NC + at_c, "op": at_y}

    def remote(src, dst, send, recv, where):
        return pltpu.make_async_remote_copy(
            src_ref=src, dst_ref=dst, send_sem=send, recv_sem=recv, device_id=where, device_id_type=MESH
        )

    twin = device(dc=1)
    near = {"z+": device(dz=1), "z-": device(dz=-1), "x+": device(dx=1), "x-": device(dx=-1)}
    links = {"z+": 0, "z-": 1, "x+": 2, "x-": 3}

    psi_load = pltpu.make_async_copy(psi_hbm, psi, load_sem.at[0])
    psi_load.start()
    kry_load = pltpu.make_async_copy(kry_hbm, kry, load_sem.at[1])
    kry_load.start()

    barrier = pltpu.get_barrier_semaphore()
    peers = [device(dy=dy, dc=dc) for dy in range(NY) for dc in range(NC) if dy or dc]
    peers += [device(dx=dx) for dx in range(1, NX)] + [device(dz=dz) for dz in range(1, NZ)]
    for peer in peers:
        pl.semaphore_signal(barrier, inc=1, device_id=peer, device_id_type=MESH)
    pl.semaphore_wait(barrier, len(peers))

    for local in range(2):
        target_y = 2 * core + local
        offset = lax.rem(target_y - y + NY, NY)
        for target_core in range(NC):
            mine = (target_y == y) & (core == target_core)
            source = rpre.at[local, target_core]
            landing = rbuf.at[pl.ds(pl.multiple_of(offset * 256, 256), 256)]

            @pl.when(mine)
            def _():
                pltpu.make_async_copy(source, landing, pre_sem.at[offset]).start()

            @pl.when(jnp.logical_not(mine))
            def _():
                remote(
                    source, landing, pre_send, pre_sem.at[offset],
                    {"sec": sec - core + target_core, "op": target_y},
                ).start()

    own_l = pltpu.make_async_copy(lenv, lall.at[0], side_sem.at[0])
    own_t = pltpu.make_async_copy(tmask, tmall.at[0], side_sem.at[NY])
    own_l.start()
    own_t.start()
    sides = []
    for dy in range(1, NY):
        sides.append(remote(tmask, tmall.at[dy], side_send.at[NY + dy], side_sem.at[NY + dy], device(dy=dy)))
        sides.append(remote(lenv, lall.at[dy], side_send.at[dy], side_sem.at[dy], device(dy=dy)))
    for copy in sides:
        copy.start()

    for offset in range(NY):
        part = rbuf.at[pl.ds(offset * 256, 256)]
        pltpu.make_async_copy(part, part, pre_sem.at[offset]).wait()

    def take(kind, slot):
        dz, dx = ORDER[slot]
        whole = rbuf.at[piece(kind, slot, 2)]
        if slot:
            sem = (a_sem if kind == "A" else b_sem).at[slot]
            pltpu.make_async_copy(whole, whole, sem).wait()
        for way, parts, place in onward(kind, dz, dx):
            there = SLOT[place]
            remote(
                rbuf.at[piece(kind, slot, parts)],
                rbuf.at[piece(kind, there, parts)],
                link_send.at[links[way]],
                (a_sem if kind == "A" else b_sem).at[there],
                near[way],
            ).start()

    def half_to_twin(slot):
        remote(
            rbuf.at[pl.ds(slot * BLOCK, HALF)],
            rbuf.at[pl.ds(slot * BLOCK + HALF, HALF)],
            twin_send,
            twin_sem.at[slot],
            twin,
        ).start()

    def branch(index):
        seen = [e for step in PLAN[:index] for e in step]

        def run():
            done = list(seen)
            for kind, slot in PLAN[index]:
                take(kind, slot)
                done.append((kind, slot))
                if ("A", slot) in done and ("B", slot) in done:
                    half_to_twin(slot)

        return run

    branches = [branch(index) for index in range(BLOCKS)]

    def send_group(first):
        for dy in range(NY):
            owner = device(dy=dy)["op"]
            source = outb.at[owner, pl.ds(first, GROUP)]
            landing = recvb.at[pl.ds(dy * BLOCKS + first, GROUP)]
            group = first // GROUP
            if dy == 0:
                pltpu.make_async_copy(source, landing, out_sem.at[0, group]).start()
            else:
                remote(source, landing, out_send, out_sem.at[dy, group], device(dy=dy)).start()

    def product(slot, carry):
        for index, run in enumerate(branches):
            if PLAN[index]:
                pl.when(slot == index)(run)

        @pl.when(slot == 0)
        def _():
            psi_load.wait()
            own_l.wait()
            own_t.wait()
            for copy in sides:
                copy.wait_recv()

        base = pl.multiple_of(slot * BLOCK, BLOCK)
        other = rbuf.at[pl.ds(base + HALF, HALF)]
        pltpu.make_async_copy(other, other, twin_sem.at[slot]).wait()
        s = tab[slot]
        a = tab[BLOCKS + slot]
        block = psi[s]
        total = jnp.zeros((TILE, TILE), jnp.float32)
        for dy in range(NY):
            weights = tmall[dy, pl.ds(s, 1), :]
            for part in range(2):
                left = lall[dy, a, pl.ds(part * 256, 256), :]
                made = jnp.dot(left, block, preferred_element_type=jnp.float32)
                pair = []
                for which in range(2):
                    lane = part * 2 + which
                    weight = jnp.broadcast_to(weights[:, lane : lane + 1], (TILE, TILE))
                    pair.append((made[which * TILE : (which + 1) * TILE] * weight).astype(jnp.bfloat16))
                start = pl.multiple_of(base + part * HALF + dy * 256, 256)
                first = rbuf[pl.ds(start, TILE), :]
                second = rbuf[pl.ds(start + TILE, TILE), :]
                total = total + lax.dot_general(
                    jnp.concatenate(pair, axis=1),
                    jnp.concatenate([first, second], axis=1),
                    (((1,), (1,)), ((), ())),
                    preferred_element_type=jnp.float32,
                )
        result = total.astype(jnp.bfloat16)
        rows = TILE // NY
        for owner in range(NY):
            outb[owner, slot] = result[owner * rows : (owner + 1) * rows]

        @pl.when(lax.rem(slot, GROUP) == GROUP - 1)
        def _():
            send_group(slot - (GROUP - 1))

        return carry

    lax.fori_loop(0, BLOCKS, product, 0)

    kry_load.wait()
    for dy in range(NY):
        for group in range(BLOCKS // GROUP):
            landing = recvb.at[pl.ds(dy * BLOCKS + group * GROUP, GROUP)]
            pltpu.make_async_copy(landing, landing, out_sem.at[dy, group]).wait()

    vectors = kry.shape[0]

    def collect(s, accs):
        rows = recvb[tab[2 * BLOCKS + s]]
        applied[s] = rows
        wide = rows.astype(jnp.float32)
        return tuple(accs[k] + kry[k, s].astype(jnp.float32) * wide for k in range(vectors))

    zero = jnp.zeros((TILE // NY, TILE), jnp.float32)
    accs = lax.fori_loop(0, psi.shape[0], collect, (zero,) * vectors)
    flat = [jnp.sum(acc, axis=0, keepdims=True) for acc in accs]
    flat += [jnp.zeros((8 - vectors, TILE), jnp.float32)]
    held = jnp.concatenate(flat, axis=0)

    stages = (
        (gather_y, y * NC + core, [(device(dy=dy, dc=dc)) for dy in range(NY) for dc in range(NC) if dy or dc]),
        (gather_x, x, [device(dx=dx) for dx in range(1, NX)]),
        (gather_z, z, [device(dz=dz) for dz in range(1, NZ)]),
    )
    for stage, (gather, place, targets) in enumerate(stages):
        sums[stage] = held
        gather[place] = held
        for target in targets:
            remote(sums.at[stage], gather.at[place], sum_send.at[stage], sum_sem.at[stage], target).start()
        most = gather.at[pl.ds(0, len(targets))]
        pltpu.make_async_copy(most, most, sum_sem.at[stage]).wait()
        held = jnp.sum(gather[...], axis=0)
    corr[...] = jnp.broadcast_to(jnp.sum(held, axis=1, keepdims=True), corr.shape)

    def sent(ref, sem):
        pltpu.make_async_copy(ref, ref, sem).wait()

    totals = dict.fromkeys(links, 0)
    for kind in ("A", "B"):
        for dz, dx in ORDER:
            for way, parts, _ in onward(kind, dz, dx):
                totals[way] += SPLIT[kind][1] * (2 if parts == 2 else 1)
    for way, rows in totals.items():
        sent(rbuf.at[pl.ds(0, rows)], link_send.at[links[way]])
    sent(rbuf.at[pl.ds(0, BLOCKS * HALF)], twin_send)
    for copy in sides:
        copy.wait_send()
    sent(recvb.at[pl.ds(0, (NY - 1) * BLOCKS)], out_send)
    for stage, (gather, place, targets) in enumerate(stages):
        sent(gather.at[pl.ds(0, len(targets))], sum_send.at[stage])
    any_mine = (y // 2) == core

    @pl.when(any_mine)
    def _():
        sent(rbuf.at[pl.ds(0, 3 * 256)], pre_send)

    @pl.when(jnp.logical_not(any_mine))
    def _():
        sent(rbuf.at[pl.ds(0, 4 * 256)], pre_send)


def per_device(
    wavefunction,
    sector_left,
    sector_right,
    left_sizes,
    right_sizes,
    term_mask,
    left_environment,
    right_environment,
    krylov_basis,
):
    sec = lax.axis_index("sec")
    y = lax.axis_index("op")
    z, x, core = sec // (NX * NC), (sec // NC) % NX, sec % NC
    sectors = wavefunction.shape[0]
    terms, left_per = left_environment.shape[:2]
    right_per = right_environment.shape[1]
    lane = jnp.arange(TILE, dtype=jnp.int32)

    places = jnp.array(ORDER, dtype=jnp.int32)
    chips = ((z + places[:, 0] + NZ) % NZ) * NX + (x + places[:, 1] + NX) % NX
    numbers = chips * NY + y
    my_right = lax.dynamic_slice_in_dim(sector_right, sec * sectors, sectors)
    match = numbers[:, None] == my_right[None, :]
    sector_at = jnp.arange(sectors, dtype=jnp.int32)
    s_of = jnp.sum(jnp.where(match, sector_at[None, :], 0), axis=1)
    a_of = jnp.sum(jnp.where(match, (sector_left - sec * left_per)[None, :], 0), axis=1)
    same_chip = (my_right // NY)[:, None] == chips[None, :]
    use_of = jnp.sum(jnp.where(same_chip, jnp.arange(BLOCKS, dtype=jnp.int32)[None, :], 0), axis=1)
    slot_of = ((y - my_right % NY + NY) % NY) * BLOCKS + use_of
    tab = jnp.concatenate([s_of, a_of, slot_of]).astype(jnp.int32)

    left_size = lax.dynamic_slice_in_dim(left_sizes, sec * left_per, left_per)
    right_size = lax.dynamic_slice_in_dim(right_sizes, sec * right_per, right_per)
    left_in = lane[None, :] < left_size[:, None]
    right_in = lane[None, :] < right_size[:, None]
    none = jnp.zeros((), jnp.bfloat16)
    left = jnp.where((left_in[:, :, None] & left_in[:, None, :])[None], left_environment, none)
    right = jnp.where((right_in[:, :, None] & right_in[:, None, :])[None], right_environment, none)
    halves = left.reshape(2, 2, left_per, TILE, TILE)
    halves = jnp.where(core == 0, halves, halves[::-1])
    lenv = halves.reshape(terms, left_per, TILE, TILE).transpose(1, 0, 2, 3).reshape(left_per, terms * TILE, TILE)
    rpre = right.reshape(2, 2, right_per, TILE, TILE).transpose(2, 0, 1, 3, 4).reshape(right_per, 2, 2 * TILE, TILE)
    mask = term_mask.reshape(2, 2, sectors)
    mask = jnp.where(core == 0, mask, mask[::-1]).reshape(terms, sectors)
    tmask = jnp.pad(mask.T.astype(jnp.float32), ((0, 0), (0, TILE - terms)))

    rows = TILE // NY
    vectors = krylov_basis.shape[0]
    dma = pltpu.SemaphoreType.DMA
    vmem = pl.BlockSpec(memory_space=pltpu.VMEM)
    anywhere = pl.BlockSpec(memory_space=pl.ANY)
    applied, corr = pl.pallas_call(
        kernel,
        name="bond_apply",
        out_shape=(
            jax.ShapeDtypeStruct((sectors, rows, TILE), jnp.bfloat16),
            jax.ShapeDtypeStruct((8, TILE), jnp.float32),
        ),
        in_specs=[pl.BlockSpec(memory_space=pltpu.SMEM), vmem, vmem, vmem, anywhere, anywhere],
        out_specs=(vmem, vmem),
        scratch_shapes=[
            pltpu.VMEM((BLOCKS * BLOCK, TILE), jnp.bfloat16),
            pltpu.VMEM((sectors, TILE, TILE), jnp.bfloat16),
            pltpu.VMEM((vectors, sectors, rows, TILE), jnp.bfloat16),
            pltpu.VMEM((NY, left_per, terms * TILE, TILE), jnp.bfloat16),
            pltpu.VMEM((NY, sectors, TILE), jnp.float32),
            pltpu.VMEM((NY, BLOCKS, rows, TILE), jnp.bfloat16),
            pltpu.VMEM((NY * BLOCKS, rows, TILE), jnp.bfloat16),
            pltpu.VMEM((3, 8, TILE), jnp.float32),
            pltpu.VMEM((NZ, 8, TILE), jnp.float32),
            pltpu.VMEM((NX, 8, TILE), jnp.float32),
            pltpu.VMEM((NY * NC, 8, TILE), jnp.float32),
            dma((2,)),
            dma((NY,)),
            dma,
            dma((2 * NY,)),
            dma((2 * NY,)),
            dma((BLOCKS,)),
            dma((BLOCKS,)),
            dma((BLOCKS,)),
            dma,
            dma((4,)),
            dma((NY, BLOCKS // GROUP)),
            dma,
            dma,
            dma((3,)),
            dma((3,)),
        ],
        compiler_params=pltpu.CompilerParams(
            collective_id=0, has_side_effects=True, vmem_limit_bytes=48 * 1024 * 1024
        ),
    )(tab, lenv, rpre, tmask, wavefunction, krylov_basis)
    return applied, corr[:vectors, 0]


def solution(mesh):
    return jax.shard_map(
        per_device,
        mesh=mesh,
        in_specs=(
            P("sec", None, None),
            P("sec"),
            P(),
            P(),
            P(),
            P("op", "sec"),
            P("op", "sec", None, None),
            P("op", "sec", None, None),
            P(None, "sec", "op", None),
        ),
        out_specs=(P("sec", "op", None), P()),
        check_vma=False,
    )
```

```python
import jax
import jax.numpy as jnp
from jax import lax
from jax.experimental import pallas as pl
from jax.experimental.pallas import tpu as pltpu
from jax.sharding import PartitionSpec as P

MESH = pl.DeviceIdType.MESH
NZ, NX, NC, NY = 8, 4, 2, 4
TILE = 128
HALF = 1024
BLOCK = 2 * HALF
SPLIT = {"A": (0, 208), "B": (416, 304)}
GROUP = 4

ORDER = (
    (-1, 0), (0, -1), (0, 0), (0, 1),
    (1, 0), (-2, 0), (-1, -1), (1, -1),
    (1, 1), (0, 2), (-1, 1), (2, 0),
    (-3, 0), (2, -1), (-2, -1), (2, 1),
    (-1, 2), (1, 2), (-2, 1), (3, 0),
    (-3, -1), (3, -1), (3, 1), (-2, 2),
    (2, 2), (-3, 1), (4, 0), (4, -1),
    (4, 1), (-3, 2), (3, 2), (4, 2),
)

PLAN = (
    (("B", 2), ("A", 2), ("B", 0), ("B", 1), ("B", 3), ("B", 4), ("A", 0), ("A", 1), ("A", 3), ("A", 4), ("B", 5), ("B", 6), ("B", 10), ("B", 11), ("B", 9), ("A", 5), ("A", 7),),
    (),
    (("A", 6), ("A", 8),),
    (("B", 7), ("B", 8),),
    (("A", 9),),
    (("A", 10), ("A", 11),),
    (),
    (),
    (("B", 14), ("B", 18),),
    (("B", 12), ("B", 19),),
    (("B", 16),),
    (("A", 12), ("A", 13),),
    (("B", 13), ("B", 15), ("A", 14), ("A", 15),),
    (("B", 17), ("A", 16), ("A", 17),),
    (("B", 23),),
    (),
    (("A", 18), ("A", 19),),
    (),
    (("B", 26), ("B", 20), ("B", 25),),
    (("A", 21),),
    (("A", 20), ("B", 21), ("B", 22), ("A", 22), ("B", 24), ("A", 23),),
    (("A", 24),),
    (("A", 25), ("A", 26),),
    (("B", 27), ("B", 28), ("A", 27),),
    (("B", 29),),
    (),
    (("A", 29), ("B", 30),),
    (("A", 30), ("A", 28),),
    (("B", 31),),
    (),
    (("A", 31),),
    (),
)

SLOT = {place: index for index, place in enumerate(ORDER)}
BLOCKS = len(ORDER)


def onward(kind, dz, dx):
    out = []
    along_z = kind == "A" or dx == 0
    along_x = kind == "B" or dz == 0
    if along_z:
        if -3 <= dz <= 0:
            out.append(("z+", 2 if dz > -3 else 0, (dz - 1 if dz > -3 else 4, dx)))
        if 0 <= dz <= 3:
            out.append(("z-", 2 if dz < 3 else 1, (dz + 1, dx)))
    if along_x:
        if -1 <= dx <= 0:
            out.append(("x+", 2 if dx == 0 else 0, (dz, -1 if dx == 0 else 2)))
        if 0 <= dx <= 1:
            out.append(("x-", 2 if dx == 0 else 1, (dz, dx + 1)))
    return out


def piece(kind, slot, parts):
    first, rows = SPLIT[kind]
    start = slot * BLOCK + first + (rows if parts == 1 else 0)
    return pl.ds(start, 2 * rows if parts == 2 else rows)


def kernel(
    places, sector_left, left_sizes, right_sizes, my_right, right_rows, tmask, left_hbm, right_hbm, psi_hbm, kry_hbm,
    applied, corr,
    rbuf, psi, kry, lall, tmall, flat_mask, turned_mask, outb, recvb, sums, gather_z, gather_x, gather_y,
    load_sem, pre_sem, pre_send, side_sem, side_send, a_sem, b_sem, twin_sem, twin_send, link_send,
    out_sem, out_send, own_sem, sum_sem, sum_send,
):
    sec = lax.axis_index("sec")
    y = lax.axis_index("op")
    z = sec // (NX * NC)
    x = (sec // NC) % NX
    core = sec % NC

    def device(dz=0, dx=0, dc=0, dy=0):
        at_z = lax.rem(z + dz + NZ, NZ) if dz else z
        at_x = lax.rem(x + dx + NX, NX) if dx else x
        at_c = 1 - core if dc else core
        at_y = lax.rem(y + dy + NY, NY) if dy else y
        return {"sec": (at_z * NX + at_x) * NC + at_c, "op": at_y}

    def remote(src, dst, send, recv, where):
        return pltpu.make_async_remote_copy(
            src_ref=src, dst_ref=dst, send_sem=send, recv_sem=recv, device_id=where, device_id_type=MESH
        )

    terms, left_per = left_hbm.shape[:2]
    twin = device(dc=1)
    near = {"z+": device(dz=1), "z-": device(dz=-1), "x+": device(dx=1), "x-": device(dx=-1)}
    links = {"z+": 0, "z-": 1, "x+": 2, "x-": 3}

    psi_load = pltpu.make_async_copy(psi_hbm, psi, load_sem.at[0])
    psi_load.start()
    kry_load = pltpu.make_async_copy(kry_hbm, kry, load_sem.at[1])
    kry_load.start()

    barrier = pltpu.get_barrier_semaphore()
    peers = [device(dy=dy, dc=dc) for dy in range(NY) for dc in range(NC) if dy or dc]
    peers += [device(dx=dx) for dx in range(1, NX)] + [device(dz=dz) for dz in range(1, NZ)]
    for peer in peers:
        pl.semaphore_signal(barrier, inc=1, device_id=peer, device_id_type=MESH)
    pl.semaphore_wait(barrier, len(peers))

    for local in range(2):
        target_y = 2 * core + local
        offset = lax.rem(target_y - y + NY, NY)
        for target_core, which in ((0, 0), (0, 1), (1, 0), (1, 1)):
            mine = (target_y == y) & (core == target_core)
            source = right_hbm.at[2 * target_core + which, local]
            start = SLOT[0, 0] * BLOCK + which * TILE + offset * 256
            landing = rbuf.at[pl.ds(pl.multiple_of(start, TILE), TILE)]

            @pl.when(mine)
            def _():
                pltpu.make_async_copy(source, landing, pre_sem.at[offset]).start()

            @pl.when(jnp.logical_not(mine))
            def _():
                remote(
                    source, landing, pre_send, pre_sem.at[offset],
                    {"sec": sec - core + target_core, "op": target_y},
                ).start()

    own_l = pltpu.make_async_copy(left_hbm, lall.at[0], side_sem.at[0])
    own_t = pltpu.make_async_copy(tmask, tmall.at[0], side_sem.at[NY])
    own_l.start()
    own_t.start()
    sides = []
    for dy in range(1, NY):
        sides.append(remote(tmask, tmall.at[dy], side_send.at[NY + dy], side_sem.at[NY + dy], device(dy=dy)))
        sides.append(remote(left_hbm, lall.at[dy], side_send.at[dy], side_sem.at[dy], device(dy=dy)))
    for copy in sides:
        copy.start()

    for offset in range(NY):
        part = rbuf.at[pl.ds(SLOT[0, 0] * BLOCK + offset * 256, 256)]
        pltpu.make_async_copy(part, part, pre_sem.at[offset]).wait()

    def take(kind, slot):
        dz, dx = ORDER[slot]
        whole = rbuf.at[piece(kind, slot, 2)]
        if dz or dx:
            sem = (a_sem if kind == "A" else b_sem).at[slot]
            pltpu.make_async_copy(whole, whole, sem).wait()
        for way, parts, place in onward(kind, dz, dx):
            there = SLOT[place]
            remote(
                rbuf.at[piece(kind, slot, parts)],
                rbuf.at[piece(kind, there, parts)],
                link_send.at[links[way]],
                (a_sem if kind == "A" else b_sem).at[there],
                near[way],
            ).start()

    def half_to_twin(slot):
        remote(
            rbuf.at[pl.ds(slot * BLOCK, HALF)],
            rbuf.at[pl.ds(slot * BLOCK + HALF, HALF)],
            twin_send,
            twin_sem.at[slot],
            twin,
        ).start()

    def branch(index):
        seen = [e for step in PLAN[:index] for e in step]

        def run():
            done = list(seen)
            for kind, slot in PLAN[index]:
                take(kind, slot)
                done.append((kind, slot))
                if ("A", slot) in done and ("B", slot) in done:
                    half_to_twin(slot)

        return run

    branches = [branch(index) for index in range(BLOCKS)]

    def send_group(first):
        for dy in range(NY):
            owner = device(dy=dy)["op"]
            source = outb.at[owner, pl.ds(first, GROUP)]
            landing = recvb.at[pl.ds(dy * BLOCKS + first, GROUP)]
            group = first // GROUP
            if dy == 0:
                pltpu.make_async_copy(source, landing, out_sem.at[0, group]).start()
            else:
                remote(source, landing, out_send, out_sem.at[dy, group], device(dy=dy)).start()

    def prepare():
        psi_load.wait()
        own_l.wait()
        own_t.wait()
        for copy in sides:
            copy.wait_recv()
        down = lax.broadcasted_iota(jnp.int32, (TILE, TILE), 0)
        across = lax.broadcasted_iota(jnp.int32, (TILE, TILE), 1)
        for a in range(left_per):
            size = left_sizes[sec * left_per + a]
            inside = jnp.where((down < size) & (across < size), 1.0, 0.0).astype(jnp.bfloat16)
            for dy in range(NY):
                for term in range(terms):
                    lall[dy, term, a] = lall[dy, term, a] * inside
        flat_mask[...] = jnp.zeros_like(flat_mask)
        for dy in range(NY):
            flat_mask[dy * terms : (dy + 1) * terms, 0 : tmall.shape[2]] = tmall[dy].astype(jnp.float32)
        turned_mask[...] = flat_mask[...].T

    def product(slot, carry):
        for index, run in enumerate(branches):
            if PLAN[index]:
                pl.when(slot == index)(run)

        pl.when(slot == 0)(prepare)
        base = pl.multiple_of(slot * BLOCK, BLOCK)
        other = rbuf.at[pl.ds(base + HALF, HALF)]
        pltpu.make_async_copy(other, other, twin_sem.at[slot]).wait()
        chip = lax.rem(z + places[BLOCKS + slot], NZ) * NX + lax.rem(x + places[2 * BLOCKS + slot], NX)
        number = chip * NY + y
        row = right_rows[pl.ds(sec // 2, 1), :]
        place = lax.broadcasted_iota(jnp.int32, (1, TILE), 1) - core * (TILE // 2)
        match = (row == number) & (place >= 0) & (place < TILE // 2)
        s = jnp.max(jnp.where(match, place, 0))
        a = lax.rem(sector_left[s], left_per)
        col_in = lax.broadcasted_iota(jnp.int32, (1, TILE), 1) < right_sizes[number]
        block = psi[s] * jnp.where(col_in, 1.0, 0.0).astype(jnp.bfloat16)
        weights = turned_mask[pl.ds(s, 1), :]
        total = jnp.zeros((TILE, TILE), jnp.float32)
        for dy in range(NY):
            for part in range(2):
                left = jnp.concatenate([lall[dy, 2 * part, a], lall[dy, 2 * part + 1, a]], axis=0)
                made = jnp.dot(left, block, preferred_element_type=jnp.float32)
                pair = []
                for which in range(2):
                    lane = dy * terms + part * 2 + which
                    weight = jnp.broadcast_to(weights[:, lane : lane + 1], (TILE, TILE))
                    pair.append((made[which * TILE : (which + 1) * TILE] * weight).astype(jnp.bfloat16))
                away = HALF * (core if part == 0 else 1 - core)
                start = pl.multiple_of(base + away + dy * 256, 256)
                first = rbuf[pl.ds(start, TILE), :]
                second = rbuf[pl.ds(start + TILE, TILE), :]
                total = total + lax.dot_general(
                    jnp.concatenate(pair, axis=1),
                    jnp.concatenate([first, second], axis=1),
                    (((1,), (1,)), ((), ())),
                    preferred_element_type=jnp.float32,
                )
        total = jnp.where(col_in, total, 0.0)
        result = total.astype(jnp.bfloat16)
        rows = TILE // NY
        for owner in range(NY):
            outb[owner, slot] = result[owner * rows : (owner + 1) * rows]

        @pl.when(lax.rem(slot, GROUP) == GROUP - 1)
        def _():
            send_group(slot - (GROUP - 1))

        return carry

    lax.fori_loop(0, BLOCKS, product, 0)

    kry_load.wait()
    for dy in range(NY):
        for group in range(BLOCKS // GROUP):
            landing = recvb.at[pl.ds(dy * BLOCKS + group * GROUP, GROUP)]
            pltpu.make_async_copy(landing, landing, out_sem.at[dy, group]).wait()

    vectors = kry.shape[0]

    def collect(s, accs):
        number = my_right[sec * psi.shape[0] + s]
        chip = number // NY
        away_z = lax.rem(chip // NX - z + NZ, NZ)
        away_x = lax.rem(chip % NX - x + NX, NX)
        plane = lax.rem(y - number % NY + NY, NY)
        rows = recvb[plane * BLOCKS + places[away_z * NX + away_x]]
        applied[s] = rows
        wide = rows.astype(jnp.float32)
        return tuple(accs[k] + kry[k, s].astype(jnp.float32) * wide for k in range(vectors))

    zero = jnp.zeros((TILE // NY, TILE), jnp.float32)
    accs = lax.fori_loop(0, psi.shape[0], collect, (zero,) * vectors, unroll=4)
    flat = [jnp.sum(acc, axis=0, keepdims=True) for acc in accs]
    flat += [jnp.zeros((8 - vectors, TILE), jnp.float32)]
    held = jnp.concatenate(flat, axis=0)

    stages = (
        (gather_y, y * NC + core, [(device(dy=dy, dc=dc)) for dy in range(NY) for dc in range(NC) if dy or dc]),
        (gather_x, x, [device(dx=dx) for dx in range(1, NX)]),
        (gather_z, z, [device(dz=dz) for dz in range(1, NZ)]),
    )
    for stage, (gather, place, targets) in enumerate(stages):
        sums[stage] = held
        gather[place] = held
        for target in targets:
            remote(sums.at[stage], gather.at[place], sum_send.at[stage], sum_sem.at[stage], target).start()
        most = gather.at[pl.ds(0, len(targets))]
        pltpu.make_async_copy(most, most, sum_sem.at[stage]).wait()
        held = jnp.sum(gather[...], axis=0)
    corr[...] = jnp.broadcast_to(jnp.sum(held, axis=1, keepdims=True), corr.shape)

    def sent(ref, sem):
        pltpu.make_async_copy(ref, ref, sem).wait()

    totals = dict.fromkeys(links, 0)
    for kind in ("A", "B"):
        for dz, dx in ORDER:
            for way, parts, _ in onward(kind, dz, dx):
                totals[way] += SPLIT[kind][1] * (2 if parts == 2 else 1)
    for way, rows in totals.items():
        sent(rbuf.at[pl.ds(0, rows)], link_send.at[links[way]])
    sent(rbuf.at[pl.ds(0, BLOCKS * HALF)], twin_send)
    for copy in sides:
        copy.wait_send()
    sent(recvb.at[pl.ds(0, (NY - 1) * BLOCKS)], out_send)
    for stage, (gather, place, targets) in enumerate(stages):
        sent(gather.at[pl.ds(0, len(targets))], sum_send.at[stage])
    any_mine = (y // 2) == core

    @pl.when(any_mine)
    def _():
        sent(rbuf.at[pl.ds(0, 3 * 256)], pre_send)

    @pl.when(jnp.logical_not(any_mine))
    def _():
        sent(rbuf.at[pl.ds(0, 4 * 256)], pre_send)


def per_device(
    wavefunction,
    sector_left,
    sector_right,
    left_sizes,
    right_sizes,
    term_mask,
    left_environment,
    right_environment,
    krylov_basis,
):
    sectors = wavefunction.shape[0]
    terms, left_per = left_environment.shape[:2]
    by_place = [SLOT[(dz + 3) % NZ - 3, (dx + 1) % NX - 1] for dz in range(NZ) for dx in range(NX)]
    places = by_place + [dz % NZ for dz, _ in ORDER] + [dx % NX for _, dx in ORDER]
    places = jnp.array(places, dtype=jnp.int32)

    rows = TILE // NY
    vectors = krylov_basis.shape[0]
    dma = pltpu.SemaphoreType.DMA
    vmem = pl.BlockSpec(memory_space=pltpu.VMEM)
    smem = pl.BlockSpec(memory_space=pltpu.SMEM)
    anywhere = pl.BlockSpec(memory_space=pl.ANY)
    applied, corr = pl.pallas_call(
        kernel,
        name="bond_apply",
        out_shape=(
            jax.ShapeDtypeStruct((sectors, rows, TILE), jnp.bfloat16),
            jax.ShapeDtypeStruct((8, TILE), jnp.float32),
        ),
        in_specs=[smem] * 5 + [vmem] * 2 + [anywhere] * 4,
        out_specs=(vmem, vmem),
        scratch_shapes=[
            pltpu.VMEM((BLOCKS * BLOCK, TILE), jnp.bfloat16),
            pltpu.VMEM((sectors, TILE, TILE), jnp.bfloat16),
            pltpu.VMEM((vectors, sectors, rows, TILE), jnp.bfloat16),
            pltpu.VMEM((NY, terms, left_per, TILE, TILE), jnp.bfloat16),
            pltpu.VMEM((NY, terms, sectors), jnp.int32),
            pltpu.VMEM((TILE, TILE), jnp.float32),
            pltpu.VMEM((TILE, TILE), jnp.float32),
            pltpu.VMEM((NY, BLOCKS, rows, TILE), jnp.bfloat16),
            pltpu.VMEM((NY * BLOCKS, rows, TILE), jnp.bfloat16),
            pltpu.VMEM((3, 8, TILE), jnp.float32),
            pltpu.VMEM((NZ, 8, TILE), jnp.float32),
            pltpu.VMEM((NX, 8, TILE), jnp.float32),
            pltpu.VMEM((NY * NC, 8, TILE), jnp.float32),
            dma((2,)),
            dma((NY,)),
            dma,
            dma((2 * NY,)),
            dma((2 * NY,)),
            dma((BLOCKS,)),
            dma((BLOCKS,)),
            dma((BLOCKS,)),
            dma,
            dma((4,)),
            dma((NY, BLOCKS // GROUP)),
            dma,
            dma,
            dma((3,)),
            dma((3,)),
        ],
        compiler_params=pltpu.CompilerParams(
            collective_id=0, has_side_effects=True, vmem_limit_bytes=60 * 1024 * 1024
        ),
    )(
        places,
        sector_left,
        left_sizes,
        right_sizes,
        sector_right,
        sector_right.reshape(-1, TILE),
        term_mask,
        left_environment,
        right_environment,
        wavefunction,
        krylov_basis,
    )
    return applied, corr[:vectors, 0]


def solution(mesh):
    return jax.shard_map(
        per_device,
        mesh=mesh,
        in_specs=(
            P("sec", None, None),
            P("sec"),
            P(),
            P(),
            P(),
            P("op", "sec"),
            P("op", "sec", None, None),
            P("op", "sec", None, None),
            P(None, "sec", "op", None),
        ),
        out_specs=(P("sec", "op", None), P()),
        check_vma=False,
    )
```
